768 devices in a mesh: dp: 24 (over z_lo, x), vocab: 32 (over y, z_hi, core).
Axes of the slice: x: 4, y: 8, z: 12 (z_hi: 2, z_lo: 6; z = z_hi * 6 + z_lo), core: 2. Of those that a mesh axis runs over, the one named last changes fastest.
Arguments:
- hidden: bfloat16 [768, 4608], P('dp'), may hold values from -18 to 18
- weight: bfloat16 [4608, 76032], P('dp', 'vocab'), may hold values from -1 to 1
- targets: int32 [768], replicated, may hold values from 0 to 76031
- advantage: float32 [768], replicated, may hold values from -4 to 4
- counts: int32 [192], replicated, may hold values from 0 to 4
- block_order: int32 [192], replicated, may hold values from 0 to 191, each once
Outputs:
- logprob: float32 [768], P('dp')
- hidden_grad: bfloat16 [768, 4608], P('vocab', 'dp')
The draws below stay inside these ranges and needn't reach their ends.
All inputs are finite; a program needn't handle non-finite values.
Results may differ from the reference program's by a relative error of at most 0.0049.
Values may be sent and summed in bfloat16 or wider, within the bound.
No kernel may reach another device: no remote copies, remote signals or barrier semaphores. Data moves between devices by JAX's collectives and lax.ppermute only.
A program may use at most 32 MiB of HBM per device.

```python
import math
import jax
import jax.numpy as jnp
import numpy as np

D = 4608
BLK = 4
RT = 768
NBLK = 192
VOCAB = 76032


group_count = 4


shared_mix = 0.8


own_mix = 0.6


def group_of(base, index):
    return jax.random.randint(jax.random.fold_in(jax.random.fold_in(base, index), 5), (), 0, group_count)


def column_signs(base, index):
    own = jax.random.rademacher(jax.random.fold_in(base, index), (D,), dtype=jnp.float32)
    shared_key = jax.random.fold_in(jax.random.fold_in(base, 977), group_of(base, index))
    shared = jax.random.rademacher(shared_key, (D,), dtype=jnp.float32)
    return (shared_mix * shared + own_mix * own) * (1.0 / math.sqrt(D))


def draw_weight(key, part):
    base = jax.random.fold_in(key, 11)
    columns = jax.vmap(lambda index: column_signs(base, index))(jnp.arange(VOCAB, dtype=jnp.int32))
    return columns.T.astype(jnp.bfloat16)


def draw_hidden(key, part):
    local = jax.random.fold_in(key, 23)
    return jnp.clip(jax.random.normal(local, (RT, D), jnp.float32), -6.0, 6.0).astype(jnp.bfloat16)


def plant(values, key, low, largest):
    index_at = [jax.random.randint(jax.random.fold_in(key, axis), (), 0, length) for axis, length in enumerate(values.shape)]
    main_axis = values.shape.index(max(values.shape))
    neighbour = index_at[:main_axis] + [(index_at[main_axis] + 1) % values.shape[main_axis]] + index_at[main_axis + 1:]
    return values.at[tuple(index_at)].set(low).at[tuple(neighbour)].set(largest)


def wide_ids(stream_key, extent, number_of, lean):
    loads = [min(1 << octave, number_of + 1 - (1 << octave)) * (1 << 20) // math.isqrt((1 << octave) ** lean) + 1 for octave in range((number_of + 1).bit_length()) if 1 << octave <= number_of]
    width = 1 + sum(loads) // (1 << 30)
    grid = np.cumsum(np.array([max(1, weight // width) for weight in loads]))
    ticket = jax.random.randint(jax.random.fold_in(stream_key, 1), extent, 0, int(grid[len(loads) - 1]))
    start = jnp.left_shift(1, jnp.searchsorted(jnp.asarray(grid, jnp.int32), ticket, side="right").astype(jnp.int32))
    rank = start - 1 + jax.random.randint(jax.random.fold_in(stream_key, 4), extent, 0, 1 << 30) % jnp.minimum(start, number_of + 1 - start)
    return jax.random.permutation(jax.random.fold_in(stream_key, 2), number_of)[rank].astype(jnp.int32)


def bell_draw(stream_key, dims, deviation, reach, held_as=jnp.bfloat16):
    array = jax.random.normal(stream_key, dims, jnp.float32) * deviation
    return jnp.minimum(jnp.maximum(array, -reach), reach).astype(held_as)


def setup_inputs(seed: int = 0) -> dict:
    keys = jax.random.split(jax.random.key(seed), 7)
    hidden = draw_hidden(jax.random.fold_in(keys[6], 71), 0)
    weight = draw_weight(jax.random.fold_in(keys[6], 71), 0)
    targets = plant(wide_ids(keys[2], (RT,), VOCAB, 2), jax.random.fold_in(keys[2], 3), 0, VOCAB - 1).astype(jnp.int32)
    advantage = bell_draw(keys[3], (RT,), 1.0, 4.0, jnp.float32)
    counts = plant(jax.random.randint(keys[4], (NBLK,), 0, BLK + 1), jax.random.fold_in(keys[4], 1), 0, BLK).astype(jnp.int32)
    block_order = jax.random.permutation(keys[5], NBLK).astype(jnp.int32)
    return dict(hidden=hidden, weight=weight, targets=targets, advantage=advantage, counts=counts, block_order=block_order)


def reference(hidden, weight, targets, advantage, counts, block_order):
    position = jnp.arange(RT, dtype=jnp.int32)
    blocks = block_order[position // BLK]
    source = (blocks * BLK + position % BLK).astype(jnp.int32)
    rows = hidden[source]
    logits = jnp.dot(rows, weight, preferred_element_type=jnp.float32)
    top = jnp.max(logits, axis=1)
    lse = top + jnp.log(jnp.sum(jnp.exp(logits - top[:, None]), axis=1))
    wanted = targets[source]
    hit = wanted[:, None] == jnp.arange(VOCAB, dtype=jnp.int32)[None, :]
    target_logit = jnp.sum(jnp.where(hit, logits, jnp.float32(0.0)), axis=1)
    logprob = target_logit - lse
    alive = (position % BLK) < counts[blocks]
    coef = jnp.where(alive, advantage[source], jnp.float32(0.0))
    probs = jnp.exp(logits - lse[:, None])
    grad_logits = (coef[:, None] * (probs - hit.astype(jnp.float32))).astype(jnp.bfloat16)
    hidden_grad = jnp.dot(grad_logits, weight.T, preferred_element_type=jnp.float32).astype(jnp.bfloat16)
    return logprob, hidden_grad
```

```python
import jax
import jax.numpy as jnp
from jax import lax
from jax.sharding import Mesh, PartitionSpec as P

BLK = 4
NZ, NX, NY, NH, NC = 6, 4, 8, 2, 2
VOC = ("y", "zh", "c")
NV = NY * NH * NC
F32, BF16 = jnp.float32, jnp.bfloat16


def roll_to(a, axis, start):
    return lax.dynamic_slice_in_dim(jnp.concatenate([a, a], axis), start, a.shape[axis], axis)


def split3(a):
    hi = lax.reduce_precision(a, 8, 7)
    rest = a - hi
    mid = lax.reduce_precision(rest, 8, 7)
    return jnp.stack([hi, mid, rest - mid], axis=1).astype(BF16)


def join3(cols):
    cols = cols.astype(F32)
    return (cols[:, 0] + cols[:, 1]) + cols[:, 2]


def line_scatter(part):
    right = left = None
    for s in range(1, NZ):
        to_right = part[NZ - s] if right is None else part[NZ - s] + right
        to_left = part[s] if left is None else part[s] + left
        right = lax.ppermute(to_right, "zl", [(i, i + 1) for i in range(s)])
        left = lax.ppermute(to_left, "zl", [(i, i - 1) for i in range(NZ - s, NZ)])
    return part[0] + right + left


def line_gather(block):
    right, left = [block], [block]
    for s in range(1, NZ):
        right.append(lax.ppermute(right[-1], "zl", [(i, i + 1) for i in range(s - 1, NZ - 1)]))
        left.append(lax.ppermute(left[-1], "zl", [(i, i - 1) for i in range(1, NZ - s + 1)]))
    z = lax.axis_index("zl")
    return [block] + [jnp.where(z >= q, right[q], left[NZ - q]) for q in range(1, NZ)]


def body(hidden, weight, targets, advantage, counts, block_order):
    per, model = hidden.shape
    feats, width = weight.shape
    rows = targets.shape[0]
    z, x = lax.axis_index("zl"), lax.axis_index("x")
    v = lax.axis_index(VOC)
    back = [(i, (i - 1) % NX) for i in range(NX)]
    forth = [(i, (i + 1) % NX) for i in range(NX)]

    half = feats // 2
    w1 = lax.ppermute(weight, "x", back)
    w3 = lax.ppermute(weight, "x", forth)
    w2 = jnp.concatenate(
        [lax.ppermute(w1[:half], "x", back), lax.ppermute(w3[half:], "x", forth)], 0
    )
    w = [weight, w1, w2, w3]

    h = hidden.reshape(per, NZ, NX, feats).transpose(1, 2, 0, 3)
    h = lax.all_to_all(h, "zl", split_axis=0, concat_axis=0, tiled=True)
    h = roll_to(roll_to(h, 1, x), 0, z)

    position = jnp.arange(rows, dtype=jnp.int32)
    blocks = block_order[position // BLK]
    source = blocks * BLK + position % BLK
    wanted = targets[source]
    alive = position % BLK < counts[blocks]
    coef = jnp.where(alive, advantage[source], F32(0.0))

    columns = v * width + jnp.arange(width, dtype=jnp.int32)
    onehot = (wanted[:, None] == columns[None, :]).astype(BF16)
    picked = lax.dot_general(onehot, weight, (((1,), (1,)), ((), ())), preferred_element_type=F32)
    share = rows // NV
    picked, h = lax.optimization_barrier((picked.astype(BF16), h))
    picked = lax.all_to_all(
        picked.reshape(NV, share, feats), VOC, split_axis=0, concat_axis=0, tiled=True
    )
    target_w = jnp.sum(picked.astype(F32), axis=0)

    part = None
    for o in (0, 1, 3, 2):
        d = jnp.dot(h[:, o].reshape(NZ * per, feats), w[o], preferred_element_type=F32)
        part = d if part is None else part + d
    logits = line_scatter(part.reshape(NZ, per, width))

    mine = lax.dynamic_slice_in_dim(targets, (z * NX + x) * per, per, 0)
    top = jnp.max(logits, axis=1)
    e = jnp.exp(logits - top[:, None])
    total = jnp.sum(e, axis=1)
    hit = mine[:, None] == columns[None, :]
    goal = jnp.sum(jnp.where(hit, logits, F32(0.0)), axis=1)

    lanes = -(-width // 128) * 128
    pad = lanes - width - 9
    sent = jnp.concatenate(
        [e.astype(BF16), split3(top), split3(total), split3(goal), jnp.zeros((per, pad), BF16)], 1
    )
    got = jnp.concatenate(line_gather(sent), 0)
    probs = got[:, :width]
    stats = [join3(got[:, width + 3 * k : width + 3 * k + 3]) for k in range(3)]
    stats = jnp.stack(stats + [jnp.zeros_like(stats[0])] * (64 - 3), axis=1)

    pieces = []
    for o in range(NX):
        g = lax.dot_general(probs, w[o], (((1,), (1,)), ((), ())), preferred_element_type=F32)
        g = jnp.concatenate([g, stats], axis=1)
        if o:
            g = lax.ppermute(g, "x", [(i, (i + o) % NX) for i in range(NX)])
        pieces.append(g)
    grads = jnp.concatenate(pieces, 0)

    owner = source // per
    place = ((x - owner % NX) % NX) * (NZ * per) + ((z - owner // NX) % NZ) * per + source % per
    grads = jnp.take(grads, place, axis=0, mode="clip")
    st = grads[:, feats : feats + 3].T
    dp_rows = lax.dynamic_slice_in_dim(st, (z * NX + x) * per, per, 1)
    extra = jnp.concatenate(
        [
            jnp.pad(st[:2].reshape(2, NV, share).transpose(1, 0, 2), ((0, 0), (0, 0), (0, feats - share))),
            jnp.broadcast_to(jnp.pad(dp_rows, ((0, 3), (0, feats - per)))[None], (NV, 6, feats)),
        ],
        axis=1,
    )
    msg = jnp.concatenate([grads[:, :feats].reshape(NV, share, feats), extra], axis=1)
    msg = lax.all_to_all(msg, VOC, split_axis=0, concat_axis=0, tiled=True)

    tops, totals = msg[:, share, :share], msg[:, share + 1, :share]
    peak = jnp.max(tops, axis=0)
    scale = jnp.exp(tops - peak[None])
    norm = jnp.sum(scale * totals, axis=0)
    mixed = jnp.sum(scale[:, :, None] * msg[:, :share], axis=0) / norm[:, None]
    my_coef = lax.dynamic_slice_in_dim(coef, v * share, share, 0)
    hidden_grad = my_coef[:, None] * (mixed - target_w)

    tops, totals, goals = (msg[:, share + 2 + k, :per] for k in range(3))
    peak = jnp.max(tops, axis=0)
    norm = jnp.sum(jnp.exp(tops - peak[None]) * totals, axis=0)
    logprob = jnp.sum(goals, axis=0) - (peak + jnp.log(norm))
    return (logprob, hidden_grad.astype(BF16))


def solution(mesh):
    fine = Mesh(mesh.devices.reshape(NZ, NX, NY, NH, NC), ("zl", "x") + VOC)
    dp = ("zl", "x")
    placed = (P(dp, None), P(dp, VOC), P(), P(), P(), P())
    return jax.shard_map(
        body, mesh=fine, in_specs=placed, out_specs=(P(dp), P(VOC, dp)), check_vma=False
    )
```

```python
import jax
import jax.numpy as jnp
from jax import lax
from jax.sharding import Mesh, PartitionSpec as P

BLK = 4
NZ, NX, NY, NH, NC = 6, 4, 8, 2, 2
VOC = ("y", "zh", "c")
NV = NY * NH * NC
F32, BF16 = jnp.float32, jnp.bfloat16


def trade(a, axes):
    return lax.all_to_all(a, axes, split_axis=0, concat_axis=0, tiled=True)


def roll_to(a, axis, start):
    return lax.dynamic_slice_in_dim(jnp.concatenate([a, a], axis), start, a.shape[axis], axis)


def stat_lanes(stats, lanes):
    lane = lax.broadcasted_iota(jnp.int32, (stats[0].shape[0], lanes), 1)
    value = jnp.zeros(lane.shape, F32)
    for k, a in enumerate(stats):
        value = jnp.where(lane // 3 == k, a[:, None], value)
    hi = lax.reduce_precision(value, 8, 7)
    rest = value - hi
    mid = lax.reduce_precision(rest, 8, 7)
    return jnp.where(lane % 3 == 0, hi, jnp.where(lane % 3 == 1, mid, rest - mid)).astype(BF16)


def join3(cols):
    cols = cols.astype(F32)
    return (cols[:, 0] + cols[:, 1]) + cols[:, 2]


def line_scatter(part):
    right = left = None
    for s in range(1, NZ):
        to_right = part[NZ - s] if right is None else part[NZ - s] + right
        to_left = part[s] if left is None else part[s] + left
        to_right, to_left = lax.optimization_barrier((to_right, to_left))
        right = lax.ppermute(to_right, "zl", [(i, i + 1) for i in range(s)])
        left = lax.ppermute(to_left, "zl", [(i, i - 1) for i in range(NZ - s, NZ)])
    return part[0] + right + left


def line_gather(block):
    right, left = [block], [block]
    for s in range(1, NZ):
        r = lax.ppermute(right[-1], "zl", [(i, i + 1) for i in range(s - 1, NZ - 1)])
        l = lax.ppermute(left[-1], "zl", [(i, i - 1) for i in range(1, NZ - s + 1)])
        r, l = lax.optimization_barrier((r, l))
        right.append(r)
        left.append(l)
    z = lax.axis_index("zl")
    return [block] + [jnp.where(z >= q, right[q], left[NZ - q]) for q in range(1, NZ)]


def merge(a, b, feats):
    top = jnp.maximum(a[:, feats], b[:, feats])[:, None]
    fa, fb = jnp.exp(a[:, feats : feats + 1] - top), jnp.exp(b[:, feats : feats + 1] - top)
    summed = fa * a + fb * b
    goal = a[:, feats + 2] + b[:, feats + 2]
    return summed[:, :feats], top[:, 0], summed[:, feats + 1], goal


def body(hidden, weight, targets, advantage, counts, block_order):
    per, _ = hidden.shape
    feats, width = weight.shape
    rows = targets.shape[0]
    z, x, core = lax.axis_index("zl"), lax.axis_index("x"), lax.axis_index("c")
    v = lax.axis_index(VOC)
    share = rows // NV
    back = [(i, (i - 1) % NX) for i in range(NX)]
    forth = [(i, (i + 1) % NX) for i in range(NX)]
    swap = [(0, 1), (1, 0)]

    half = feats // 2
    up, down = weight[:half], weight[half:]
    u1, d3 = lax.ppermute(up, "x", back), lax.ppermute(down, "x", forth)
    d1, u3 = lax.ppermute(down, "x", back), lax.ppermute(up, "x", forth)
    u2, d2 = lax.ppermute(u1, "x", back), lax.ppermute(d3, "x", forth)
    w = [weight] + [jnp.concatenate(p, 0) for p in ((u1, d1), (u2, d2), (u3, d3))]

    h = hidden.reshape(per, NZ, NX, feats).transpose(1, 2, 0, 3)
    h = trade(h, "zl")
    h = roll_to(roll_to(h, 1, x), 0, z)

    k = jnp.arange(rows // NC, dtype=jnp.int32)
    pair = (k // share) * (NC * share) + k % share
    position = jnp.concatenate([pair + (1 - core) * share, pair + core * share])
    blocks = block_order[position // BLK]
    source = blocks * BLK + position % BLK
    wanted = targets[source]

    columns = v * width + jnp.arange(width, dtype=jnp.int32)
    onehot = (wanted[:, None] == columns[None, :]).astype(BF16)
    picked = lax.dot_general(onehot, weight, (((1,), (1,)), ((), ())), preferred_element_type=F32)
    picked = picked.astype(BF16)
    picked = picked[rows // NC :] + lax.ppermute(picked[: rows // NC], "c", swap)
    picked, h = lax.optimization_barrier((picked, h))
    picked = trade(picked.reshape(NY * NH, share, feats), ("y", "zh"))

    part = None
    for o in (0, 1, 3, 2):
        d = jnp.dot(h[:, o].reshape(NZ * per, feats), w[o], preferred_element_type=F32)
        part = d if part is None else part + d
    logits = line_scatter(part.reshape(NZ, per, width))

    mine = lax.dynamic_slice_in_dim(targets, (z * NX + x) * per, per, 0)
    top = jnp.max(logits, axis=1)
    e = jnp.exp(logits - top[:, None])
    total = jnp.sum(e, axis=1)
    hit = mine[:, None] == columns[None, :]
    goal = jnp.sum(jnp.where(hit, logits, F32(0.0)), axis=1)

    lanes = -(-width // 128) * 128
    sent = jnp.concatenate(
        [e.astype(BF16), stat_lanes((top, total, goal), lanes - width)], 1
    )
    got = jnp.concatenate(line_gather(sent), 0)
    probs = got[:, :width]
    stats = [join3(got[:, width + 3 * k : width + 3 * k + 3]) for k in range(3)]
    stats = jnp.stack(stats + [jnp.zeros_like(stats[0])] * (64 - 3), axis=1)

    pieces = [None] * NX
    for o in (2, 1, 3, 0):
        g = lax.dot_general(probs, w[o], (((1,), (1,)), ((), ())), preferred_element_type=F32)
        g = jnp.concatenate([g, stats], axis=1)
        pieces[o] = lax.ppermute(g, "x", [(i, (i + o) % NX) for i in range(NX)]) if o else g
    grads = jnp.concatenate(pieces, 0)

    here = (z * NX + x) * per
    own = here + jnp.arange(per, dtype=jnp.int32)
    own = block_order[own // BLK] * BLK + own % BLK
    order = jnp.concatenate([source[: rows // NC], own, source[rows // NC :], own])
    owner = order // per
    place = ((x - owner % NX) % NX) * (NZ * per) + ((z - owner // NX) % NZ) * per + order % per
    grads = jnp.take(grads, place, axis=0, mode="clip")
    cut = rows // NC + per
    grads, top, total, goal = merge(
        grads[cut:], lax.ppermute(grads[:cut], "c", swap), feats
    )
    nd = NY * NH
    kept = rows // NC
    by_dest = jnp.stack([a[:kept].reshape(nd, share) for a in (top, total)], axis=1)
    by_dest = jnp.pad(by_dest, ((0, 0), (0, 0), (0, feats - share)))
    by_row = jnp.stack([a[kept:] for a in (top, total, goal)])
    by_row = jnp.broadcast_to(jnp.pad(by_row, ((0, 3), (0, feats - per)))[None], (nd, 6, feats))
    msg = jnp.concatenate([grads[:kept].reshape(nd, share, feats), by_dest, by_row], axis=1)
    msg = lax.all_to_all(msg, ("y", "zh"), split_axis=0, concat_axis=0, tiled=True)

    spot = v * share + jnp.arange(share, dtype=jnp.int32)
    block = block_order[spot // BLK]
    alive = spot % BLK < counts[block]
    coef = jnp.where(alive, advantage[block * BLK + spot % BLK], F32(0.0))

    tops, totals = msg[:, share, :share], msg[:, share + 1, :share]
    peak = jnp.max(tops, axis=0)
    scale = jnp.exp(tops - peak[None])
    norm = jnp.sum(scale * totals, axis=0)
    mixed = jnp.sum(scale[:, :, None] * msg[:, :share], axis=0) / norm[:, None]
    target_w = jnp.sum(picked.astype(F32), axis=0)
    hidden_grad = coef[:, None] * (mixed - target_w)

    tops, totals, goals = (msg[:, share + 2 + k, :per] for k in range(3))
    peak = jnp.max(tops, axis=0)
    norm = jnp.sum(jnp.exp(tops - peak[None]) * totals, axis=0)
    logprob = jnp.sum(goals, axis=0) - (peak + jnp.log(norm))
    return (logprob, hidden_grad.astype(BF16))


def solution(mesh):
    fine = Mesh(mesh.devices.reshape(NZ, NX, NY, NH, NC), ("zl", "x") + VOC)
    dp = ("zl", "x")
    placed = (P(dp, None), P(dp, VOC), P(), P(), P(), P())

    return jax.shard_map(
        body, mesh=fine, in_specs=placed, out_specs=(P(dp), P(VOC, dp)), check_vma=False
    )
```

```python
import jax
import jax.numpy as jnp
from jax import lax
from jax.sharding import Mesh, PartitionSpec as P

BLK = 4
NA, NB, NX, NY, NH, NC = 3, 2, 4, 8, 2, 2
NZ = NA * NB
VOC = ("y", "zh", "c")
LINE = ("za", "zb")
NV = NY * NH * NC
F32, BF16 = jnp.float32, jnp.bfloat16


def trade(a, axes):
    return lax.all_to_all(a, axes, split_axis=0, concat_axis=0, tiled=True)


def roll_to(a, axis, start):
    return lax.dynamic_slice_in_dim(jnp.concatenate([a, a], axis), start, a.shape[axis], axis)


def stat_lanes(stats, lanes):
    lane = lax.broadcasted_iota(jnp.int32, (stats[0].shape[0], lanes), 1)
    value = jnp.zeros(lane.shape, F32)
    for k, a in enumerate(stats):
        value = jnp.where(lane // 3 == k, a[:, None], value)
    hi = lax.reduce_precision(value, 8, 7)
    rest = value - hi
    mid = lax.reduce_precision(rest, 8, 7)
    return jnp.where(lane % 3 == 0, hi, jnp.where(lane % 3 == 1, mid, rest - mid)).astype(BF16)


def join3(cols):
    cols = cols.astype(F32)
    return (cols[:, 0] + cols[:, 1]) + cols[:, 2]


def merge(a, b, feats):
    top = jnp.maximum(a[:, feats], b[:, feats])[:, None]
    fa, fb = jnp.exp(a[:, feats : feats + 1] - top), jnp.exp(b[:, feats : feats + 1] - top)
    summed = fa * a + fb * b
    goal = a[:, feats + 2] + b[:, feats + 2]
    return summed[:, :feats], top[:, 0], summed[:, feats + 1], goal


def body(hidden, weight, targets, advantage, counts, block_order):
    per, _ = hidden.shape
    feats, width = weight.shape
    rows = targets.shape[0]
    z, x, core = lax.axis_index(LINE), lax.axis_index("x"), lax.axis_index("c")
    v = lax.axis_index(VOC)
    share = rows // NV
    back = [(i, (i - 1) % NX) for i in range(NX)]
    forth = [(i, (i + 1) % NX) for i in range(NX)]
    swap = [(0, 1), (1, 0)]

    half = feats // 2
    up, down = weight[:half], weight[half:]
    u1, d3 = lax.ppermute(up, "x", back), lax.ppermute(down, "x", forth)
    d1, u3 = lax.ppermute(down, "x", back), lax.ppermute(up, "x", forth)
    u2, d2 = lax.ppermute(u1, "x", back), lax.ppermute(d3, "x", forth)
    w = [(0, 0, up), (0, half, down), (1, 0, u1), (1, half, d1)]
    w += [(3, 0, u3), (3, half, d3), (2, 0, u2), (2, half, d2)]

    h = hidden.reshape(per, NZ, NX * 2, half).transpose(1, 2, 0, 3)
    h = trade(h, LINE).reshape(NA, NB, NX, 2, per, half).transpose(1, 2, 3, 0, 4, 5)
    h = roll_to(roll_to(h, 1, x), 0, 1 - lax.axis_index("zb"))

    k = jnp.arange(rows // NC, dtype=jnp.int32)
    pair = (k // share) * (NC * share) + k % share
    position = jnp.concatenate([pair + (1 - core) * share, pair + core * share])
    blocks = block_order[position // BLK]
    source = blocks * BLK + position % BLK
    wanted = targets[source]

    columns = v * width + jnp.arange(width, dtype=jnp.int32)
    onehot = (wanted[:, None] == columns[None, :]).astype(BF16)
    picked = lax.dot_general(
        onehot, weight, (((1,), (1,)), ((), ())), preferred_element_type=F32
    ).astype(BF16)
    picked = picked[rows // NC :] + lax.ppermute(picked[: rows // NC], "c", swap)

    parts = []
    for r in range(NB):
        part = None
        for o, first, rows_w in w:
            d = jnp.dot(
                h[r, o, first // half].reshape(NA * per, half), rows_w, preferred_element_type=F32
            )
            part = d if part is None else part + d
        parts.append(part)
    logits = parts[1] + lax.ppermute(parts[0], "zb", swap)
    logits = jnp.sum(trade(logits.reshape(NA, per, width), "za"), axis=0)

    mine = lax.dynamic_slice_in_dim(targets, (z * NX + x) * per, per, 0)
    top = jnp.max(logits, axis=1)
    e = jnp.exp(logits - top[:, None])
    total = jnp.sum(e, axis=1)
    hit = mine[:, None] == columns[None, :]
    goal = jnp.sum(jnp.where(hit, logits, F32(0.0)), axis=1)

    lanes = -(-width // 128) * 128
    sent = jnp.concatenate(
        [e.astype(BF16), stat_lanes((top, total, goal), lanes - width)], 1
    )
    got = trade(jnp.broadcast_to(sent[None], (NZ, per, lanes)), LINE)
    got = got.reshape(NZ * per, lanes)
    probs = got[:, :width]
    stats = [join3(got[:, width + 3 * k : width + 3 * k + 3]) for k in range(3)]
    stats = jnp.stack(stats + [jnp.zeros_like(stats[0])] * (64 - 3), axis=1)

    pieces = [None] * NX
    for o in (2, 1, 3, 0):
        g = [
            lax.dot_general(probs, m, (((1,), (1,)), ((), ())), preferred_element_type=F32)
            for p, _, m in w
            if p == o
        ]
        g = jnp.concatenate(g + [stats], axis=1)
        pieces[o] = lax.ppermute(g, "x", [(i, (i + o) % NX) for i in range(NX)]) if o else g
    grads = jnp.concatenate(pieces, 0)

    here = (z * NX + x) * per
    own = here + jnp.arange(per, dtype=jnp.int32)
    own = block_order[own // BLK] * BLK + own % BLK
    order = jnp.concatenate([source[: rows // NC], own, source[rows // NC :], own])
    owner = order // per
    place = ((x - owner % NX) % NX) * (NZ * per) + (owner // NX) * per + order % per
    grads = jnp.take(grads, place, axis=0, mode="clip")
    cut = rows // NC + per
    grads, top, total, goal = merge(
        grads[cut:], lax.ppermute(grads[:cut], "c", swap), feats
    )
    kept, wide = rows // NC, NH * share
    lines = [a[:kept].reshape(NY, 1, wide) for a in (top, total)]
    lines += [jnp.broadcast_to(a[kept:].reshape(1, 1, per), (NY, 1, per)) for a in (top, total, goal)]
    lines = [jnp.pad(a, ((0, 0), (0, 0), (0, feats - a.shape[2]))) for a in lines]
    lines.append(jnp.zeros((NY, 3, feats), F32))
    blocks_of = [a.reshape(NY, wide, feats) for a in (grads[:kept], picked.astype(F32))]
    msg = trade(jnp.concatenate(blocks_of + lines, axis=1), "y")

    def over(tops, totals):
        peak = jnp.max(tops, axis=0)
        scale = jnp.exp(tops - peak[None])
        return scale, peak, jnp.sum(scale * totals, axis=0)

    base = 2 * wide
    scale, top, total = over(msg[:, base, :wide], msg[:, base + 1, :wide])
    mixed = jnp.sum(scale[:, :, None] * msg[:, :wide], axis=0)
    target_w = jnp.sum(msg[:, wide:base], axis=0)
    _, row_top, row_total = over(msg[:, base + 2, :per], msg[:, base + 3, :per])
    row_goal = jnp.sum(msg[:, base + 4, :per], axis=0)

    def half_of(side):
        pick = lambda a: lax.dynamic_index_in_dim(a.reshape((NH, share) + a.shape[1:]), side, 0, False)
        lines = [pick(top), pick(total), row_top, row_total, row_goal]
        lines = [jnp.pad(a, (0, feats - a.shape[0]))[None] for a in lines]
        return jnp.concatenate([pick(mixed), pick(target_w)] + lines + [jnp.zeros((3, feats), F32)], 0)

    zh = lax.axis_index("zh")
    far = lax.ppermute(half_of(1 - zh), "zh", swap)
    both = jnp.stack([half_of(zh), far])

    spot = v * share + jnp.arange(share, dtype=jnp.int32)
    block = block_order[spot // BLK]
    alive = spot % BLK < counts[block]
    coef = jnp.where(alive, advantage[block * BLK + spot % BLK], F32(0.0))

    base = 2 * share
    scale, _, norm = over(both[:, base, :share], both[:, base + 1, :share])
    mixed = jnp.sum(scale[:, :, None] * both[:, :share], axis=0) / norm[:, None]
    hidden_grad = coef[:, None] * (mixed - jnp.sum(both[:, share:base], axis=0))
    _, peak, norm = over(both[:, base + 2, :per], both[:, base + 3, :per])
    logprob = jnp.sum(both[:, base + 4, :per], axis=0) - (peak + jnp.log(norm))
    return (logprob, hidden_grad.astype(BF16))


def solution(mesh):
    fine = Mesh(mesh.devices.reshape(NA, NB, NX, NY, NH, NC), LINE + ("x",) + VOC)
    dp = LINE + ("x",)
    placed = (P(dp, None), P(dp, VOC), P(), P(), P(), P())

    return jax.shard_map(
        body, mesh=fine, in_specs=placed, out_specs=(P(dp), P(VOC, dp)), check_vma=False
    )
```
